32 devices in a mesh: span: 8 (over y, x, core), wall: 4 (over z).
Axes of the slice: x: 2, y: 2, z: 4, core: 2. Of those that a mesh axis runs over, the one named last changes fastest.
Arguments:
- moments: float32 [4, 64, 512, 128], P(None, 'span', 'wall'), may hold values from -32 to 32, as said below
- diffusivity: float32 [64, 512, 128], P('span', 'wall'), may hold values from 0.05 to 20
Outputs:
- transported: float32 [4, 64, 512, 128], P(None, 'span', 'wall')
- updated: float32 [4, 64, 512, 128], P(None, 'span', 'wall')
The draws below stay inside these ranges and needn't reach their ends.
Inputs may be any that keep to these rules, and one draw needn't show every extreme that they name: `moments`: in every cell m_k = w_1 u_1^k + w_2 u_2^k for k = 0..3, with weights w_1, w_2 between 0.5 and 2 and abscissas u_1, u_2 between -2 and 2 that differ by 0.5 or more.
All inputs are finite; a program needn't handle non-finite values.
Results may differ from the reference program's by a relative error of at most 0.0025.
Values sent between devices are 32-bit elements; how exact they have to be, the bound alone decides.
A program may use at most 64 MiB of HBM per device.

```python
import math
import jax
import jax.numpy as jnp
from jax import lax

NY = 512
NZ = 128
NX = 64


def draw_moments(key, part):
    keys_all = jax.random.split(jax.random.fold_in(key, 17), 4)
    shape_cells = (NX, NY, NZ)
    weight_low = jnp.exp(jax.random.uniform(keys_all[0], shape_cells, jnp.float32, jnp.log(0.5), jnp.log(2.0)))
    weight_high = jnp.exp(jax.random.uniform(keys_all[1], shape_cells, jnp.float32, jnp.log(0.5), jnp.log(2.0)))
    centre = jax.random.uniform(keys_all[2], shape_cells, jnp.float32, -1.0, 1.0)
    half_gap = jax.random.uniform(keys_all[3], shape_cells, jnp.float32, 0.25, 1.0)
    abscissa_low = centre - half_gap
    abscissa_high = centre + half_gap
    layers = []
    power_low = jnp.ones_like(centre)
    power_high = jnp.ones_like(centre)
    for order_index in range(4):
        layers.append(weight_low * power_low + weight_high * power_high)
        power_low = power_low * abscissa_low
        power_high = power_high * abscissa_high
    return jnp.stack(layers).astype(jnp.float32)


def steps_of(own_key, extent, pieces, least, largest):
    level, own = 1.0, jax.random.fold_in(own_key, 6)
    for position, shards_of in pieces:
        heights = jnp.exp(jax.random.uniform(jax.random.fold_in(own, position), (shards_of,), jnp.float32, least / len(pieces), largest / len(pieces)))
        level = level * jnp.repeat(heights, extent[position] // shards_of).reshape([-1 if axis == position else 1 for axis in range(len(extent))])
    return level


def setup_inputs(seed: int = 0) -> dict:
    splits = jax.random.split(jax.random.key(seed), 3)
    moments = draw_moments(jax.random.fold_in(splits[2], 71), 0)
    diffusivity = jnp.clip(jnp.exp(math.log(20.0) - 5.9914645 * jax.random.uniform(splits[1], (NX, NY, NZ), jnp.float32) ** steps_of(splits[1], (NX, NY, NZ), ((0, 8), (1, 4)), -0.2, 0.2)), 0.05, 20.0)
    return dict(moments=moments, diffusivity=diffusivity)


courant = 0.2
diffusion_number = 20000.0

def quadrature(moments):
    moment_zero = moments[0]
    moment_one = moments[1]
    moment_two = moments[2]
    moment_three = moments[3]
    mean_speed = moment_one / moment_zero
    ratio_two = moment_two / moment_zero
    central_two = ratio_two - mean_speed * mean_speed
    central_three = moment_three / moment_zero - 3.0 * mean_speed * ratio_two + 2.0 * mean_speed * mean_speed * mean_speed
    skewness = central_three / central_two
    radius = jnp.sqrt(0.25 * skewness * skewness + central_two)
    root_low = 0.5 * skewness - radius
    root_high = 0.5 * skewness + radius
    weight_low = moment_zero * root_high / (2.0 * radius)
    weight_high = -moment_zero * root_low / (2.0 * radius)
    return jnp.stack([weight_low, weight_high, mean_speed + root_low, mean_speed + root_high])

def minmod(first_diff, second_diff):
    return jnp.maximum(jnp.minimum(first_diff, second_diff), 0.0) + jnp.minimum(jnp.maximum(first_diff, second_diff), 0.0)

def directed(state, outgoing):
    node_terms = []
    for node_index in range(2):
        weight_node = state[node_index]
        abscissa = state[node_index + 2]
        if outgoing:
            carried = jnp.maximum(abscissa, 0.0)
        else:
            carried = jnp.minimum(abscissa, 0.0)
        carried_mass = weight_node * carried
        node_terms.append([carried_mass, carried_mass * abscissa, carried_mass * abscissa * abscissa, carried_mass * abscissa * abscissa * abscissa])
    return jnp.stack([node_terms[0][power_index] + node_terms[1][power_index] for power_index in range(4)])

def thomas(rhs_moments, diffusivity):
    lower = jnp.concatenate([jnp.zeros_like(diffusivity[:, :1, :]), diffusivity[:, :-1, :]], axis=1)
    sub_diag = -diffusion_number * lower
    super_diag = -diffusion_number * diffusivity
    main_diag = 1.0 + diffusion_number * lower + diffusion_number * diffusivity
    sub_rows = jnp.moveaxis(sub_diag, 1, 0)
    main_rows = jnp.moveaxis(main_diag, 1, 0)
    super_rows = jnp.moveaxis(super_diag, 1, 0)
    rhs_rows = jnp.moveaxis(rhs_moments, 2, 0)

    def forward(carry, row_data):
        prev_link, prev_value = carry
        sub_row, main_row, super_row, rhs_row = row_data
        denominator = main_row - sub_row * prev_link
        new_link = super_row / denominator
        new_value = (rhs_row - sub_row[None] * prev_value) / denominator[None]
        return ((new_link, new_value), (new_link, new_value))
    start = (jnp.zeros_like(main_rows[0]), jnp.zeros_like(rhs_rows[0]))
    _, (links, values) = lax.scan(forward, start, (sub_rows, main_rows, super_rows, rhs_rows))

    def backward(next_value, row_data):
        link_row, value_row = row_data
        solved_row = value_row - link_row[None] * next_value
        return (solved_row, solved_row)
    _, solved = lax.scan(backward, jnp.zeros_like(rhs_rows[0]), (links, values), reverse=True)
    return jnp.moveaxis(solved, 0, 2)

def reference(moments, diffusivity):
    quad_nodes = quadrature(moments)
    forward_diff = jnp.roll(quad_nodes, -1, axis=1) - quad_nodes
    backward_diff = quad_nodes - jnp.roll(quad_nodes, 1, axis=1)
    limited_slope = minmod(forward_diff, backward_diff)
    upper_state = quad_nodes + 0.5 * limited_slope
    lower_state = quad_nodes - 0.5 * limited_slope
    face_flux = directed(upper_state, True) + jnp.roll(directed(lower_state, False), -1, axis=1)
    transported = moments - courant * (face_flux - jnp.roll(face_flux, 1, axis=1))
    updated = thomas(transported, diffusivity)
    return (transported, updated)
```

```python
import functools

import jax
import jax.numpy as jnp
from jax import lax
from jax.experimental import pallas as pl
from jax.experimental.pallas import tpu as pltpu
from jax.sharding import PartitionSpec as P

courant = 0.2
diffusion_number = 20000.0
VMEM_LIMIT = 60 * 1024 * 1024


def quadrature(m0, m1, m2, m3):
    inverse = 1.0 / m0
    mean = m1 * inverse
    ratio_two = m2 * inverse
    central_two = ratio_two - mean * mean
    central_three = m3 * inverse - 3.0 * mean * ratio_two + 2.0 * mean * mean * mean
    half_skew = 0.5 * (central_three / central_two)
    square = half_skew * half_skew + central_two
    inverse_root = lax.rsqrt(square)
    root = square * inverse_root
    scale = m0 * (0.5 * inverse_root)
    low = half_skew - root
    high = half_skew + root
    return (scale * high, -scale * low, mean + low, mean + high)


def half_slope(below, centre, above):
    first = above - centre
    second = centre - below
    return 0.5 * (
        jnp.maximum(jnp.minimum(first, second), 0.0) + jnp.minimum(jnp.maximum(first, second), 0.0)
    )


def directed(state, outgoing):
    total = None
    for node in range(2):
        speed = state[node + 2]
        carried = jnp.maximum(speed, 0.0) if outgoing else jnp.minimum(speed, 0.0)
        term = state[node] * carried
        terms = [term]
        for _ in range(3):
            term = term * speed
            terms.append(term)
        total = terms if total is None else [a + b for a, b in zip(total, terms)]
    return total


def transport_kernel(
    n_span, n_wall, chunk,
    m_hbm, k_hbm,
    ts, hs, us, vs, ends,
    ms, lo, hi, ks, coef_g, rhs_g, starts,
    own_sem, halo_send, halo_recv, coef_send, coef_recv, rhs_send, rhs_recv,
):
    planes, rows, width = m_hbm.shape[1], m_hbm.shape[2], m_hbm.shape[3]
    pitch = ts.shape[1] // planes
    chunks = rows // chunk
    me_s = lax.axis_index("span")
    me_w = lax.axis_index("wall")
    right = lax.rem(me_s + 1, n_span)
    left = lax.rem(me_s + n_span - 1, n_span)

    own_k = pltpu.make_async_copy(k_hbm, ks.reshape(planes, pitch, width).at[:, pl.ds(0, rows), :], own_sem.at[0])
    own_k.start()
    own_m = pltpu.make_async_copy(m_hbm, ms, own_sem.at[1])
    own_m.start()

    barrier = pltpu.get_barrier_semaphore()
    for other in (left, right):
        pl.semaphore_signal(barrier, inc=1, device_id={"span": other}, device_id_type=pl.DeviceIdType.MESH)
    for step in range(1, n_wall):
        pl.semaphore_signal(
            barrier, inc=1, device_id={"wall": lax.rem(me_w + step, n_wall)}, device_id_type=pl.DeviceIdType.MESH
        )
    pl.semaphore_wait(barrier, n_wall + 1)

    def halo_copy(side, c):
        at = pl.ds(pl.multiple_of(c * chunk, 8), chunk)
        first = planes - 2 if side == 0 else 0
        return pltpu.make_async_remote_copy(
            src_ref=m_hbm.at[:, pl.ds(first, 2), at, :],
            dst_ref=(lo if side == 0 else hi).at[:, :, at, :],
            send_sem=halo_send.at[side, c],
            recv_sem=halo_recv.at[side, c],
            device_id={"span": right if side == 0 else left},
            device_id_type=pl.DeviceIdType.MESH,
        )

    def wall_copy(buffer, send, recv, step):
        return pltpu.make_async_remote_copy(
            src_ref=buffer.at[me_w],
            dst_ref=buffer.at[me_w],
            send_sem=send.at[step - 1],
            recv_sem=recv.at[step - 1],
            device_id={"wall": lax.rem(me_w + step, n_wall)},
            device_id_type=pl.DeviceIdType.MESH,
        )

    def start_halo(c, _):
        halo_copy(0, c).start()
        halo_copy(1, c).start()
        return 0

    lax.fori_loop(0, chunks, start_halo, 0)

    own_k.wait()
    zero = jnp.zeros((planes, width), jnp.float32)
    one = jnp.ones((planes, width), jnp.float32)

    def line_row(step, carry):
        v, phi, v_sum, u, psi, u_sum = carry
        for i in range(8):
            j = step * 8 + i
            vs[j] = v
            phi = phi + v
            v_sum = v_sum + v
            v = v + phi * (1.0 / (diffusion_number * ks[pl.ds(j, planes, stride=pitch), :]))
            b = rows - 1 - j
            psi = psi + u
            u = u + psi * (1.0 / (diffusion_number * ks[pl.ds(b, planes, stride=pitch), :]))
            us[b] = u
            u_sum = u_sum + u
        return (v, phi, v_sum, u, psi, u_sum)

    v_end, _, v_sum, u_end, _, u_sum = lax.fori_loop(
        0, rows // 8, line_row, (zero, one, zero, zero, one, zero)
    )
    through = 1.0 / v_end
    norm = 1.0 / u_end
    coef_g[me_w, 0] = through
    coef_g[me_w, 1] = u_sum * norm
    coef_g[me_w, 2] = v_sum * through
    for step in range(1, n_wall):
        wall_copy(coef_g, coef_send, coef_recv, step).start()

    def scale_row(step, _):
        for i in range(8):
            us[step * 8 + i] = us[step * 8 + i] * norm
        return 0

    lax.fori_loop(0, rows // 8, scale_row, 0)
    own_m.wait()

    def group(index, carry):
        base = pl.multiple_of(index * 8, 8)
        at = pl.ds(base, 8)

        def cell(p):
            if p < 0:
                return [lo[k, p + 2, at, :] for k in range(4)]
            if p >= planes:
                return [hi[k, p - planes, at, :] for k in range(4)]
            return [ms[k, p, at, :] for k in range(4)]

        below = None
        centre = quadrature(*cell(-2))
        above = quadrature(*cell(-1))
        going = None
        flux_before = None
        for p in range(-1, planes + 1):
            below, centre, above = centre, above, quadrature(*cell(p + 1))
            slope = [half_slope(b, c, a) for b, c, a in zip(below, centre, above)]
            if p >= 0:
                coming = directed([c - s for c, s in zip(centre, slope)], False)
                flux = [a + b for a, b in zip(going, coming)]
                if p >= 1:
                    for k in range(4):
                        ts[k, pl.ds(pl.multiple_of((p - 1) * pitch + base, 8), 8), :] = ms[k, p - 1, at, :] - courant * (
                            flux[k] - flux_before[k]
                        )
                flux_before = flux
            if p < planes:
                going = directed([c + s for c, s in zip(centre, slope)], True)
        sums_v, sums_u = list(carry[:4]), list(carry[4:])
        for i in range(8):
            v = vs[base + i]
            u = us[base + i]
            for k in range(4):
                t = ts[k, pl.ds(base + i, planes, stride=pitch), :]
                sums_v[k] = sums_v[k] + v * t
                sums_u[k] = sums_u[k] + u * t
                hs[k, base + i] = u * sums_v[k] - v * sums_u[k]
        return tuple(sums_v + sums_u)

    def chunk_step(c, carry):
        halo_copy(0, c).wait_recv()
        halo_copy(1, c).wait_recv()
        for g in range(chunk // 8):
            carry = group(c * (chunk // 8) + g, carry)
        return carry

    sums = lax.fori_loop(0, chunks, chunk_step, (zero,) * 8)
    for k in range(4):
        rhs_g[me_w, k] = sums[4 + k]
        rhs_g[me_w, 4 + k] = sums[k] * through
    for step in range(1, n_wall):
        wall_copy(rhs_g, rhs_send, rhs_recv, step).start()
    for step in range(1, n_wall):
        wall_copy(coef_g, coef_send, coef_recv, step).wait()

    links, inverses = [], []
    held = None
    for s in range(n_wall):
        link = coef_g[s, 0]
        ground = coef_g[s, 1]
        if s > 0:
            ground = ground + coef_g[s - 1, 2] + links[-1] * held * inverses[-1]
        held = ground
        links.append(link)
        inverses.append(1.0 / (held + link))

    for step in range(1, n_wall):
        wall_copy(rhs_g, rhs_send, rhs_recv, step).wait()
    for k in range(4):
        sources = []
        for s in range(n_wall):
            source = rhs_g[s, k]
            if s > 0:
                source = source + rhs_g[s - 1, 4 + k] + links[s - 1] * inverses[s - 1] * sources[-1]
            sources.append(source)
        value = zero
        starts[n_wall, k] = zero
        for s in reversed(range(n_wall)):
            value = (sources[s] + links[s] * value) * inverses[s]
            starts[s, k] = value
    for k in range(4):
        ends[k] = starts[me_w, k]
        ends[4 + k] = sums[4 + k] + through * starts[me_w + 1, k]

    def end_halo(c, _):
        halo_copy(0, c).wait_send()
        halo_copy(1, c).wait_send()
        return 0

    lax.fori_loop(0, chunks, end_halo, 0)


def output_kernel(parts, ts, hs, us, vs, ends, t_hbm, x_hbm, xs, t_sem, x_sem):
    planes, rows, width = t_hbm.shape[1], t_hbm.shape[2], t_hbm.shape[3]
    pitch = ts.shape[1] // planes
    size = rows // parts
    moved = pltpu.make_async_copy(
        ts.reshape(4, planes, pitch, width).at[:, :, pl.ds(0, rows), :], t_hbm, t_sem.at[0]
    )
    moved.start()
    copies = []
    for part in range(parts):

        def row_block(step, _):
            for i in range(8):
                j = part * size + step * 8 + i
                v = vs[j]
                u = us[j]
                for k in range(4):
                    xs[k, pl.ds(j, planes, stride=pitch), :] = hs[k, j] + (u * ends[k] + v * ends[4 + k])
            return 0

        lax.fori_loop(0, size // 8, row_block, 0)
        at = pl.ds(part * size, size)
        copy = pltpu.make_async_copy(
            xs.reshape(4, planes, pitch, width).at[:, :, at, :], x_hbm.at[:, :, at, :], x_sem.at[part]
        )
        copy.start()
        copies.append(copy)
    moved.wait()
    for copy in copies:
        copy.wait()


def body(n_span, n_wall, moments, diffusivity):
    _, planes, rows, width = moments.shape
    pitch = rows + 8
    chunk = 16 if rows % 16 == 0 else 8
    f32 = jnp.float32
    dma = pltpu.SemaphoreType.DMA
    any_spec = pl.BlockSpec(memory_space=pl.ANY)
    vmem_spec = pl.BlockSpec(memory_space=pltpu.VMEM)
    middle = [
        (4, planes * pitch, width),
        (4, rows, planes, width),
        (rows, planes, width),
        (rows, planes, width),
        (8, planes, width),
    ]
    held = pl.pallas_call(
        functools.partial(transport_kernel, n_span, n_wall, chunk),
        out_shape=[pltpu.VMEM(shape, f32) for shape in middle],
        in_specs=[pl.BlockSpec(memory_space=pltpu.HBM)] * 2,
        out_specs=[vmem_spec] * 5,
        scratch_shapes=[
            pltpu.VMEM((4, planes, rows, width), f32),
            pltpu.VMEM((4, 2, rows, width), f32),
            pltpu.VMEM((4, 2, rows, width), f32),
            pltpu.VMEM((planes * pitch, width), f32),
            pltpu.VMEM((n_wall, 3, planes, width), f32),
            pltpu.VMEM((n_wall, 8, planes, width), f32),
            pltpu.VMEM((n_wall + 1, 4, planes, width), f32),
            dma((2,)),
            dma((2, rows // chunk)),
            dma((2, rows // chunk)),
            dma((n_wall - 1,)),
            dma((n_wall - 1,)),
            dma((n_wall - 1,)),
            dma((n_wall - 1,)),
        ],
        compiler_params=pltpu.CompilerParams(collective_id=0, has_side_effects=True, vmem_limit_bytes=24 << 20),
        name="transport",
    )(moments, diffusivity)
    parts = 4
    out = jax.ShapeDtypeStruct(moments.shape, f32)
    return pl.pallas_call(
        functools.partial(output_kernel, parts),
        out_shape=[out, out],
        in_specs=[vmem_spec] * 5,
        out_specs=[any_spec, any_spec],
        scratch_shapes=[pltpu.VMEM((4, planes * pitch, width), f32), dma((1,)), dma((parts,))],
        compiler_params=pltpu.CompilerParams(vmem_limit_bytes=24 << 20),
        name="outputs",
    )(*held)


def solution(mesh):
    in_specs = (P(None, "span", "wall", None), P("span", "wall", None))
    out_specs = (P(None, "span", "wall", None), P(None, "span", "wall", None))
    run = functools.partial(body, mesh.shape["span"], mesh.shape["wall"])
    return jax.shard_map(run, mesh=mesh, in_specs=in_specs, out_specs=out_specs, check_vma=False)
```

```python
import functools

import jax
import jax.numpy as jnp
from jax import lax
from jax.experimental import pallas as pl
from jax.experimental.pallas import tpu as pltpu
from jax.sharding import PartitionSpec as P

courant = 0.2
diffusion_number = 20000.0
VMEM_LIMIT = 60 * 1024 * 1024


def quadrature(m0, m1, m2, m3):
    inverse = 1.0 / m0
    mean = m1 * inverse
    ratio_two = m2 * inverse
    central_two = ratio_two - mean * mean
    central_three = m3 * inverse - 3.0 * mean * ratio_two + 2.0 * mean * mean * mean
    half_skew = 0.5 * (central_three / central_two)
    square = half_skew * half_skew + central_two
    inverse_root = lax.rsqrt(square)
    root = square * inverse_root
    scale = m0 * (0.5 * inverse_root)
    low = half_skew - root
    high = half_skew + root
    return (scale * high, -scale * low, mean + low, mean + high)


def half_slope(below, centre, above):
    first = above - centre
    second = centre - below
    return 0.5 * (
        jnp.maximum(jnp.minimum(first, second), 0.0) + jnp.minimum(jnp.maximum(first, second), 0.0)
    )


def directed(state, outgoing):
    total = None
    for node in range(2):
        speed = state[node + 2]
        carried = jnp.maximum(speed, 0.0) if outgoing else jnp.minimum(speed, 0.0)
        term = state[node] * carried
        terms = [term]
        for _ in range(3):
            term = term * speed
            terms.append(term)
        total = terms if total is None else [a + b for a, b in zip(total, terms)]
    return total


def transport_kernel(
    n_span, n_wall, chunk,
    m_hbm, k_hbm,
    ts, hs, us, vs, ends,
    ms, lo, hi, ks, coef_g, rhs_g, starts,
    own_sem, halo_send, halo_recv, coef_send, coef_recv, rhs_send, rhs_recv,
):
    planes, rows, width = m_hbm.shape[1], m_hbm.shape[2], m_hbm.shape[3]
    pitch = ts.shape[1] // planes
    chunks = rows // chunk
    me_s = lax.axis_index("span")
    me_w = lax.axis_index("wall")
    right = lax.rem(me_s + 1, n_span)
    left = lax.rem(me_s + n_span - 1, n_span)

    own_k = pltpu.make_async_copy(k_hbm, ks.reshape(planes, pitch, width).at[:, pl.ds(0, rows), :], own_sem.at[0])
    own_k.start()
    own_m = pltpu.make_async_copy(m_hbm, ms, own_sem.at[1])
    own_m.start()

    barrier = pltpu.get_barrier_semaphore()
    for other in (left, right):
        pl.semaphore_signal(barrier, inc=1, device_id={"span": other}, device_id_type=pl.DeviceIdType.MESH)
    for step in range(1, n_wall):
        pl.semaphore_signal(
            barrier, inc=1, device_id={"wall": lax.rem(me_w + step, n_wall)}, device_id_type=pl.DeviceIdType.MESH
        )
    pl.semaphore_wait(barrier, n_wall + 1)

    def halo_copy(side, c):
        at = pl.ds(pl.multiple_of(c * chunk, 8), chunk)
        first = planes - 2 if side == 0 else 0
        return pltpu.make_async_remote_copy(
            src_ref=m_hbm.at[:, pl.ds(first, 2), at, :],
            dst_ref=(lo if side == 0 else hi).at[:, :, at, :],
            send_sem=halo_send.at[side, c],
            recv_sem=halo_recv.at[side, c],
            device_id={"span": right if side == 0 else left},
            device_id_type=pl.DeviceIdType.MESH,
        )

    def wall_copy(buffer, send, recv, step):
        return pltpu.make_async_remote_copy(
            src_ref=buffer.at[me_w],
            dst_ref=buffer.at[me_w],
            send_sem=send.at[step - 1],
            recv_sem=recv.at[step - 1],
            device_id={"wall": lax.rem(me_w + step, n_wall)},
            device_id_type=pl.DeviceIdType.MESH,
        )

    def start_halo(c, _):
        halo_copy(0, c).start()
        halo_copy(1, c).start()
        return 0

    lax.fori_loop(0, chunks, start_halo, 0)

    own_k.wait()
    zero = jnp.zeros((planes, width), jnp.float32)
    one = jnp.ones((planes, width), jnp.float32)

    def line_row(step, carry):
        v, phi, v_sum, u, psi, u_sum = carry
        for i in range(8):
            j = step * 8 + i
            vs[j] = v
            phi = phi + v
            v_sum = v_sum + v
            v = v + phi * (1.0 / (diffusion_number * ks[pl.ds(j, planes, stride=pitch), :]))
            b = rows - 1 - j
            psi = psi + u
            u = u + psi * (1.0 / (diffusion_number * ks[pl.ds(b, planes, stride=pitch), :]))
            us[b] = u
            u_sum = u_sum + u
        return (v, phi, v_sum, u, psi, u_sum)

    v_end, _, v_sum, u_end, _, u_sum = lax.fori_loop(
        0, rows // 8, line_row, (zero, one, zero, zero, one, zero)
    )
    through = 1.0 / v_end
    norm = 1.0 / u_end
    coef_g[me_w, 0] = through
    coef_g[me_w, 1] = u_sum * norm
    coef_g[me_w, 2] = v_sum * through
    for step in range(1, n_wall):
        wall_copy(coef_g, coef_send, coef_recv, step).start()

    def scale_row(step, _):
        for i in range(8):
            us[step * 8 + i] = us[step * 8 + i] * norm
        return 0

    lax.fori_loop(0, rows // 8, scale_row, 0)
    own_m.wait()

    def group(index, carry):
        base = pl.multiple_of(index * 8, 8)
        at = pl.ds(base, 8)

        def cell(p):
            if p < 0:
                return [lo[k, p + 2, at, :] for k in range(4)]
            if p >= planes:
                return [hi[k, p - planes, at, :] for k in range(4)]
            return [ms[k, p, at, :] for k in range(4)]

        below = None
        centre = quadrature(*cell(-2))
        above = quadrature(*cell(-1))
        going = None
        flux_before = None
        for p in range(-1, planes + 1):
            below, centre, above = centre, above, quadrature(*cell(p + 1))
            slope = [half_slope(b, c, a) for b, c, a in zip(below, centre, above)]
            if p >= 0:
                coming = directed([c - s for c, s in zip(centre, slope)], False)
                flux = [a + b for a, b in zip(going, coming)]
                if p >= 1:
                    for k in range(4):
                        ts[k, pl.ds(pl.multiple_of((p - 1) * pitch + base, 8), 8), :] = ms[k, p - 1, at, :] - courant * (
                            flux[k] - flux_before[k]
                        )
                flux_before = flux
            if p < planes:
                going = directed([c + s for c, s in zip(centre, slope)], True)
        sums_v, sums_u = list(carry[:4]), list(carry[4:])
        for i in range(8):
            v = vs[base + i]
            u = us[base + i]
            for k in range(4):
                t = ts[k, pl.ds(base + i, planes, stride=pitch), :]
                sums_v[k] = sums_v[k] + v * t
                sums_u[k] = sums_u[k] + u * t
                hs[k, base + i] = u * sums_v[k] - v * sums_u[k]
        return tuple(sums_v + sums_u)

    def chunk_step(c, carry):
        halo_copy(0, c).wait_recv()
        halo_copy(1, c).wait_recv()
        for g in range(chunk // 8):
            carry = group(c * (chunk // 8) + g, carry)
        return carry

    sums = lax.fori_loop(0, chunks, chunk_step, (zero,) * 8)
    for k in range(4):
        rhs_g[me_w, k] = sums[4 + k]
        rhs_g[me_w, 4 + k] = sums[k] * through
    for step in range(1, n_wall):
        wall_copy(rhs_g, rhs_send, rhs_recv, step).start()
    for step in range(1, n_wall):
        wall_copy(coef_g, coef_send, coef_recv, step).wait()

    links, inverses = [], []
    held = None
    for s in range(n_wall):
        link = coef_g[s, 0]
        ground = coef_g[s, 1]
        if s > 0:
            ground = ground + coef_g[s - 1, 2] + links[-1] * held * inverses[-1]
        held = ground
        links.append(link)
        inverses.append(1.0 / (held + link))

    for step in range(1, n_wall):
        wall_copy(rhs_g, rhs_send, rhs_recv, step).wait()
    for k in range(4):
        sources = []
        for s in range(n_wall):
            source = rhs_g[s, k]
            if s > 0:
                source = source + rhs_g[s - 1, 4 + k] + links[s - 1] * inverses[s - 1] * sources[-1]
            sources.append(source)
        value = zero
        starts[n_wall, k] = zero
        for s in reversed(range(n_wall)):
            value = (sources[s] + links[s] * value) * inverses[s]
            starts[s, k] = value
    for k in range(4):
        ends[k] = starts[me_w, k]
        ends[4 + k] = sums[4 + k] + through * starts[me_w + 1, k]

    def end_halo(c, _):
        halo_copy(0, c).wait_send()
        halo_copy(1, c).wait_send()
        return 0

    lax.fori_loop(0, chunks, end_halo, 0)


def output_kernel(parts, ts, hs, us, vs, ends, t_hbm, x_hbm, xs, t_sem, x_sem):
    planes, rows, width = t_hbm.shape[1], t_hbm.shape[2], t_hbm.shape[3]
    pitch = ts.shape[1] // planes
    size = rows // parts
    moved = pltpu.make_async_copy(
        ts.reshape(4, planes, pitch, width).at[:, :, pl.ds(0, rows), :], t_hbm, t_sem.at[0]
    )
    moved.start()
    copies = []
    for part in range(parts):

        def row_block(step, _):
            for i in range(8):
                j = part * size + step * 8 + i
                v = vs[j]
                u = us[j]
                for k in range(4):
                    xs[k, pl.ds(j, planes, stride=pitch), :] = hs[k, j] + (u * ends[k] + v * ends[4 + k])
            return 0

        lax.fori_loop(0, size // 8, row_block, 0)
        at = pl.ds(part * size, size)
        copy = pltpu.make_async_copy(
            xs.reshape(4, planes, pitch, width).at[:, :, at, :], x_hbm.at[:, :, at, :], x_sem.at[part]
        )
        copy.start()
        copies.append(copy)
    moved.wait()
    for copy in copies:
        copy.wait()


def body(n_span, n_wall, moments, diffusivity):
    _, planes, rows, width = moments.shape
    pitch = rows + 8
    chunk = 16 if rows % 16 == 0 else 8
    f32 = jnp.float32
    dma = pltpu.SemaphoreType.DMA
    any_spec = pl.BlockSpec(memory_space=pl.ANY)
    vmem_spec = pl.BlockSpec(memory_space=pltpu.VMEM)
    middle = [
        (4, planes * pitch, width),
        (4, rows, planes, width),
        (rows, planes, width),
        (rows, planes, width),
        (8, planes, width),
    ]
    held = pl.pallas_call(
        functools.partial(transport_kernel, n_span, n_wall, chunk),
        out_shape=[pltpu.VMEM(shape, f32) for shape in middle],
        in_specs=[pl.BlockSpec(memory_space=pltpu.HBM)] * 2,
        out_specs=[vmem_spec] * 5,
        scratch_shapes=[
            pltpu.VMEM((4, planes, rows, width), f32),
            pltpu.VMEM((4, 2, rows, width), f32),
            pltpu.VMEM((4, 2, rows, width), f32),
            pltpu.VMEM((planes * pitch, width), f32),
            pltpu.VMEM((n_wall, 3, planes, width), f32),
            pltpu.VMEM((n_wall, 8, planes, width), f32),
            pltpu.VMEM((n_wall + 1, 4, planes, width), f32),
            dma((2,)),
            dma((2, rows // chunk)),
            dma((2, rows // chunk)),
            dma((n_wall - 1,)),
            dma((n_wall - 1,)),
            dma((n_wall - 1,)),
            dma((n_wall - 1,)),
        ],
        compiler_params=pltpu.CompilerParams(collective_id=0, has_side_effects=True, vmem_limit_bytes=24 << 20),
        name="transport",
    )(
        pltpu.with_memory_space_constraint(moments, pltpu.HBM),
        pltpu.with_memory_space_constraint(diffusivity, pltpu.HBM),
    )
    parts = 4
    out = jax.ShapeDtypeStruct(moments.shape, f32)
    return pl.pallas_call(
        functools.partial(output_kernel, parts),
        out_shape=[out, out],
        in_specs=[vmem_spec] * 5,
        out_specs=[any_spec, any_spec],
        scratch_shapes=[pltpu.VMEM((4, planes * pitch, width), f32), dma((1,)), dma((parts,))],
        compiler_params=pltpu.CompilerParams(vmem_limit_bytes=24 << 20),
        name="outputs",
    )(*held)


def solution(mesh):
    in_specs = (P(None, "span", "wall", None), P("span", "wall", None))
    out_specs = (P(None, "span", "wall", None), P(None, "span", "wall", None))
    run = functools.partial(body, mesh.shape["span"], mesh.shape["wall"])
    return jax.shard_map(run, mesh=mesh, in_specs=in_specs, out_specs=out_specs, check_vma=False)
```

```python
import functools

import jax
import jax.numpy as jnp
from jax import lax
from jax.experimental import pallas as pl
from jax.experimental.pallas import tpu as pltpu
from jax.sharding import PartitionSpec as P

courant = 0.2
diffusion_number = 20000.0
VMEM_LIMIT = 60 * 1024 * 1024


def quadrature(m0, m1, m2, m3):
    inverse = 1.0 / m0
    mean = m1 * inverse
    ratio_two = m2 * inverse
    central_two = ratio_two - mean * mean
    central_three = m3 * inverse - 3.0 * mean * ratio_two + 2.0 * mean * mean * mean
    half_skew = 0.5 * (central_three / central_two)
    square = half_skew * half_skew + central_two
    inverse_root = lax.rsqrt(square)
    root = square * inverse_root
    scale = m0 * (0.5 * inverse_root)
    low = half_skew - root
    high = half_skew + root
    return (scale * high, -scale * low, mean + low, mean + high)


def half_slope(below, centre, above):
    first = above - centre
    second = centre - below
    return 0.5 * (
        jnp.maximum(jnp.minimum(first, second), 0.0) + jnp.minimum(jnp.maximum(first, second), 0.0)
    )


def directed(state, outgoing):
    total = None
    for node in range(2):
        speed = state[node + 2]
        carried = jnp.maximum(speed, 0.0) if outgoing else jnp.minimum(speed, 0.0)
        term = state[node] * carried
        terms = [term]
        for _ in range(3):
            term = term * speed
            terms.append(term)
        total = terms if total is None else [a + b for a, b in zip(total, terms)]
    return total


def transport_kernel(
    n_span, n_wall, chunk,
    m_hbm, k_hbm,
    ts, hs, us, vs, ends,
    ms, ks, coef_g, rhs_g, starts,
    own_sem, halo_send, halo_recv, coef_send, coef_recv, rhs_send, rhs_recv,
):
    planes, rows, width = m_hbm.shape[1], m_hbm.shape[2], m_hbm.shape[3]
    pitch = ts.shape[1] // planes
    chunks = rows // chunk
    me_s = lax.axis_index("span")
    me_w = lax.axis_index("wall")
    right = lax.rem(me_s + 1, n_span)
    left = lax.rem(me_s + n_span - 1, n_span)
    late = lax.rem(me_s, 2)

    own_k = pltpu.make_async_copy(k_hbm, ks.reshape(planes, pitch, width).at[:, pl.ds(0, rows), :], own_sem.at[0])
    own_k.start()
    own_m = pltpu.make_async_copy(m_hbm, ms.at[:, pl.ds(2, planes)], own_sem.at[1])
    own_m.start()

    barrier = pltpu.get_barrier_semaphore()
    for other in (left, right):
        pl.semaphore_signal(barrier, inc=1, device_id={"span": other}, device_id_type=pl.DeviceIdType.MESH)
    for step in range(1, n_wall):
        pl.semaphore_signal(
            barrier, inc=1, device_id={"wall": lax.rem(me_w + step, n_wall)}, device_id_type=pl.DeviceIdType.MESH
        )
    pl.semaphore_wait(barrier, n_wall + 1)

    def halo_copy(side, c):
        at = pl.ds(pl.multiple_of(c * chunk, 8), chunk)
        return pltpu.make_async_remote_copy(
            src_ref=m_hbm.at[:, pl.ds((1 - side) * (planes - 2), 2), at, :],
            dst_ref=ms.at[:, pl.ds(side * (planes + 2), 2), at, :],
            send_sem=halo_send.at[side, c],
            recv_sem=halo_recv.at[side, c],
            device_id={"span": lax.rem(me_s + 1 + side * (n_span - 2), n_span)},
            device_id_type=pl.DeviceIdType.MESH,
        )

    def wall_copy(buffer, send, recv, step, *at):
        part = buffer.at[(me_w, *at)]
        return pltpu.make_async_remote_copy(
            src_ref=part,
            dst_ref=part,
            send_sem=send.at[step - 1],
            recv_sem=recv.at[step - 1],
            device_id={"wall": lax.rem(me_w + step, n_wall)},
            device_id_type=pl.DeviceIdType.MESH,
        )

    def sums_copy(stage, step):
        if stage == 0:
            at = pl.ds(pl.multiple_of((1 - late) * 16, 8), 8 * (planes - 2))
        else:
            at = pl.ds(pl.multiple_of(late * 8 * (planes - 2), 8), 16)
        return wall_copy(rhs_g, rhs_send.at[stage], rhs_recv.at[stage], step, at)

    def start_halo(c, _):
        halo_copy(1 - late, c).start()
        halo_copy(late, c).start()
        return 0

    lax.fori_loop(0, chunks, start_halo, 0)

    own_k.wait()
    zero = jnp.zeros((planes, width), jnp.float32)
    one = jnp.ones((planes, width), jnp.float32)

    def line_row(step, carry):
        v, phi, v_sum, u, psi, u_sum = carry
        for i in range(8):
            j = step * 8 + i
            vs[j] = v
            phi = phi + v
            v_sum = v_sum + v
            v = v + phi * (1.0 / (diffusion_number * ks[pl.ds(j, planes, stride=pitch), :]))
            b = rows - 1 - j
            psi = psi + u
            u = u + psi * (1.0 / (diffusion_number * ks[pl.ds(b, planes, stride=pitch), :]))
            us[b] = u
            u_sum = u_sum + u
        return (v, phi, v_sum, u, psi, u_sum)

    v_end, _, v_sum, u_end, _, u_sum = lax.fori_loop(
        0, rows // 8, line_row, (zero, one, zero, zero, one, zero)
    )
    through = 1.0 / v_end
    norm = 1.0 / u_end
    coef_g[me_w, 0] = through
    coef_g[me_w, 1] = u_sum * norm
    coef_g[me_w, 2] = v_sum * through
    for step in range(1, n_wall):
        wall_copy(coef_g, coef_send, coef_recv, step).start()

    def scale_row(step, _):
        for i in range(8):
            us[step * 8 + i] = us[step * 8 + i] * norm
        return 0

    lax.fori_loop(0, rows // 8, scale_row, 0)
    own_m.wait()

    def transport(base, first, count):
        at = pl.ds(base, 8)

        def cell(p):
            return [ms[k, first + p + 2, at, :] for k in range(4)]

        below = None
        centre = quadrature(*cell(-2))
        above = quadrature(*cell(-1))
        going = None
        flux_before = None
        for p in range(-1, count + 1):
            below, centre, above = centre, above, quadrature(*cell(p + 1))
            slope = [half_slope(b, c, a) for b, c, a in zip(below, centre, above)]
            if p >= 0:
                coming = directed([c - s for c, s in zip(centre, slope)], False)
                flux = [a + b for a, b in zip(going, coming)]
                if p >= 1:
                    row = pl.ds(pl.multiple_of((first + p - 1) * pitch + base, 8), 8)
                    for k in range(4):
                        ts[k, row, :] = ms[k, first + p + 1, at, :] - courant * (flux[k] - flux_before[k])
                flux_before = flux
            if p < count:
                going = directed([c + s for c, s in zip(centre, slope)], True)

    def add_rows(base, carry, keep):
        sums_v, sums_u = list(carry[:4]), list(carry[4:])
        for i in range(8):
            v = vs[base + i]
            u = us[base + i]
            for k in range(4):
                t = ts[k, pl.ds(base + i, planes, stride=pitch), :]
                sums_v[k] = sums_v[k] + v * t
                sums_u[k] = sums_u[k] + u * t
                if keep:
                    hs[k, base + i] = u * sums_v[k] - v * sums_u[k]
        return tuple(sums_v + sums_u)

    def pass_over(stage):
        first = (1 - late) * 2 if stage == 0 else late * (planes - 2)
        count = planes - 2 if stage == 0 else 2

        def step(c, carry):
            halo_copy(1 - late if stage == 0 else late, c).wait_recv()
            for g in range(chunk // 8):
                base = pl.multiple_of(c * chunk + g * 8, 8)
                transport(base, first, count)
                carry = add_rows(base, carry, stage == 1)
            return carry

        return lax.fori_loop(0, chunks, step, (zero,) * 8)

    def put_sums(sums):
        for k in range(4):
            rhs_g[me_w, pl.ds(k, planes, stride=8), :] = sums[4 + k]
            rhs_g[me_w, pl.ds(4 + k, planes, stride=8), :] = sums[k] * through

    put_sums(pass_over(0))
    for step in range(1, n_wall):
        sums_copy(0, step).start()
    sums = pass_over(1)
    for step in range(1, n_wall):
        sums_copy(0, step).wait()
    put_sums(sums)
    for step in range(1, n_wall):
        sums_copy(1, step).start()
    for step in range(1, n_wall):
        wall_copy(coef_g, coef_send, coef_recv, step).wait()

    links, inverses = [], []
    held = None
    for s in range(n_wall):
        link = coef_g[s, 0]
        ground = coef_g[s, 1]
        if s > 0:
            ground = ground + coef_g[s - 1, 2] + links[-1] * held * inverses[-1]
        held = ground
        links.append(link)
        inverses.append(1.0 / (held + link))

    for step in range(1, n_wall):
        sums_copy(1, step).wait()
    for k in range(4):
        sources = []
        for s in range(n_wall):
            source = rhs_g[s, pl.ds(k, planes, stride=8), :]
            if s > 0:
                source = (
                    source
                    + rhs_g[s - 1, pl.ds(4 + k, planes, stride=8), :]
                    + links[s - 1] * inverses[s - 1] * sources[-1]
                )
            sources.append(source)
        value = zero
        starts[n_wall, k] = zero
        for s in reversed(range(n_wall)):
            value = (sources[s] + links[s] * value) * inverses[s]
            starts[s, k] = value
    for k in range(4):
        ends[k] = starts[me_w, k]
        ends[4 + k] = sums[4 + k] + through * starts[me_w + 1, k]

    def end_halo(c, _):
        halo_copy(0, c).wait_send()
        halo_copy(1, c).wait_send()
        return 0

    lax.fori_loop(0, chunks, end_halo, 0)


def output_kernel(parts, ts, hs, us, vs, ends, t_hbm, x_hbm, xs, t_sem, x_sem):
    planes, rows, width = t_hbm.shape[1], t_hbm.shape[2], t_hbm.shape[3]
    pitch = ts.shape[1] // planes
    size = rows // parts
    moved = pltpu.make_async_copy(
        ts.reshape(4, planes, pitch, width).at[:, :, pl.ds(0, rows), :], t_hbm, t_sem.at[0]
    )
    moved.start()
    copies = []
    for part in range(parts):

        def row_block(step, _):
            for i in range(8):
                j = part * size + step * 8 + i
                v = vs[j]
                u = us[j]
                for k in range(4):
                    xs[k, pl.ds(j, planes, stride=pitch), :] = hs[k, j] + (u * ends[k] + v * ends[4 + k])
            return 0

        lax.fori_loop(0, size // 8, row_block, 0)
        at = pl.ds(part * size, size)
        copy = pltpu.make_async_copy(
            xs.reshape(4, planes, pitch, width).at[:, :, at, :], x_hbm.at[:, :, at, :], x_sem.at[part]
        )
        copy.start()
        copies.append(copy)
    moved.wait()
    for copy in copies:
        copy.wait()


def body(n_span, n_wall, moments, diffusivity):
    _, planes, rows, width = moments.shape
    pitch = rows + 8
    chunk = 16 if rows % 16 == 0 else 8
    f32 = jnp.float32
    dma = pltpu.SemaphoreType.DMA
    any_spec = pl.BlockSpec(memory_space=pl.ANY)
    vmem_spec = pl.BlockSpec(memory_space=pltpu.VMEM)
    middle = [
        (4, planes * pitch, width),
        (4, rows, planes, width),
        (rows, planes, width),
        (rows, planes, width),
        (8, planes, width),
    ]
    held = pl.pallas_call(
        functools.partial(transport_kernel, n_span, n_wall, chunk),
        out_shape=[pltpu.VMEM(shape, f32) for shape in middle],
        in_specs=[pl.BlockSpec(memory_space=pltpu.HBM)] * 2,
        out_specs=[vmem_spec] * 5,
        scratch_shapes=[
            pltpu.VMEM((4, planes + 4, rows, width), f32),
            pltpu.VMEM((planes * pitch, width), f32),
            pltpu.VMEM((n_wall, 3, planes, width), f32),
            pltpu.VMEM((n_wall, planes * 8, width), f32),
            pltpu.VMEM((n_wall + 1, 4, planes, width), f32),
            dma((2,)),
            dma((2, rows // chunk)),
            dma((2, rows // chunk)),
            dma((n_wall - 1,)),
            dma((n_wall - 1,)),
            dma((2, n_wall - 1)),
            dma((2, n_wall - 1)),
        ],
        compiler_params=pltpu.CompilerParams(collective_id=0, has_side_effects=True, vmem_limit_bytes=24 << 20),
        name="transport",
    )(
        pltpu.with_memory_space_constraint(moments, pltpu.HBM),
        pltpu.with_memory_space_constraint(diffusivity, pltpu.HBM),
    )
    parts = 4
    out = jax.ShapeDtypeStruct(moments.shape, f32)
    return pl.pallas_call(
        functools.partial(output_kernel, parts),
        out_shape=[out, out],
        in_specs=[vmem_spec] * 5,
        out_specs=[any_spec, any_spec],
        scratch_shapes=[pltpu.VMEM((4, planes * pitch, width), f32), dma((1,)), dma((parts,))],
        compiler_params=pltpu.CompilerParams(vmem_limit_bytes=24 << 20),
        name="outputs",
    )(*held)


def solution(mesh):
    in_specs = (P(None, "span", "wall", None), P("span", "wall", None))
    out_specs = (P(None, "span", "wall", None), P(None, "span", "wall", None))
    run = functools.partial(body, mesh.shape["span"], mesh.shape["wall"])
    return jax.shard_map(run, mesh=mesh, in_specs=in_specs, out_specs=out_specs, check_vma=False)
```

```python
import functools

import jax
import jax.numpy as jnp
from jax import lax
from jax.experimental import pallas as pl
from jax.experimental.pallas import tpu as pltpu
from jax.sharding import PartitionSpec as P

courant = 0.2
diffusion_number = 20000.0
VMEM_LIMIT = 60 * 1024 * 1024


def quadrature(m0, m1, m2, m3):
    inverse = 1.0 / m0
    mean = m1 * inverse
    ratio_two = m2 * inverse
    central_two = ratio_two - mean * mean
    central_three = m3 * inverse - 3.0 * mean * ratio_two + 2.0 * mean * mean * mean
    half_skew = 0.5 * (central_three / central_two)
    square = half_skew * half_skew + central_two
    inverse_root = lax.rsqrt(square)
    root = square * inverse_root
    scale = m0 * (0.5 * inverse_root)
    low = half_skew - root
    high = half_skew + root
    return (scale * high, -scale * low, mean + low, mean + high)


def half_slope(below, centre, above):
    first = above - centre
    second = centre - below
    return 0.5 * (
        jnp.maximum(jnp.minimum(first, second), 0.0) + jnp.minimum(jnp.maximum(first, second), 0.0)
    )


def directed(state, outgoing):
    total = None
    for node in range(2):
        speed = state[node + 2]
        carried = jnp.maximum(speed, 0.0) if outgoing else jnp.minimum(speed, 0.0)
        term = state[node] * carried
        terms = [term]
        for _ in range(3):
            term = term * speed
            terms.append(term)
        total = terms if total is None else [a + b for a, b in zip(total, terms)]
    return total


def transport_kernel(
    n_span, n_wall, chunk,
    m_hbm, k_hbm,
    ts, hs, us, vs, ends,
    ms, ks, coef_g, rhs_g, starts,
    own_sem, halo_send, halo_recv, coef_send, coef_recv, rhs_send, rhs_recv,
):
    planes, rows, width = m_hbm.shape[1], m_hbm.shape[2], m_hbm.shape[3]
    pitch = ts.shape[1] // planes
    chunks = rows // chunk
    me_s = lax.axis_index("span")
    me_w = lax.axis_index("wall")
    right = lax.rem(me_s + 1, n_span)
    left = lax.rem(me_s + n_span - 1, n_span)
    late = lax.rem(me_s, 2)

    own_k = pltpu.make_async_copy(k_hbm, ks.reshape(planes, pitch, width).at[:, pl.ds(0, rows), :], own_sem.at[0])
    own_k.start()
    own_m = pltpu.make_async_copy(m_hbm, ms.at[:, pl.ds(2, planes)], own_sem.at[1])
    own_m.start()

    barrier = pltpu.get_barrier_semaphore()
    for other in (left, right):
        pl.semaphore_signal(barrier, inc=1, device_id={"span": other}, device_id_type=pl.DeviceIdType.MESH)
    for step in range(1, n_wall):
        pl.semaphore_signal(
            barrier, inc=1, device_id={"wall": lax.rem(me_w + step, n_wall)}, device_id_type=pl.DeviceIdType.MESH
        )
    pl.semaphore_wait(barrier, n_wall + 1)

    def halo_copy(side, c):
        at = pl.ds(pl.multiple_of(c * chunk, 8), chunk)
        return pltpu.make_async_remote_copy(
            src_ref=m_hbm.at[:, pl.ds((1 - side) * (planes - 2), 2), at, :],
            dst_ref=ms.at[:, pl.ds(side * (planes + 2), 2), at, :],
            send_sem=halo_send.at[side, c],
            recv_sem=halo_recv.at[side, c],
            device_id={"span": lax.rem(me_s + 1 + side * (n_span - 2), n_span)},
            device_id_type=pl.DeviceIdType.MESH,
        )

    def wall_copy(buffer, send, recv, step, *at):
        part = buffer.at[(me_w, *at)]
        return pltpu.make_async_remote_copy(
            src_ref=part,
            dst_ref=part,
            send_sem=send.at[step - 1],
            recv_sem=recv.at[step - 1],
            device_id={"wall": lax.rem(me_w + step, n_wall)},
            device_id_type=pl.DeviceIdType.MESH,
        )

    def sums_copy(stage, step):
        if stage == 0:
            at = pl.ds(pl.multiple_of((1 - late) * 16, 8), 8 * (planes - 2))
        else:
            at = pl.ds(pl.multiple_of(late * 8 * (planes - 2), 8), 16)
        return wall_copy(rhs_g, rhs_send.at[stage], rhs_recv.at[stage], step, at)

    direct = lax.rem(lax.div(me_s, 2) + me_s, 2)

    def start_halo(side):
        def start(c, _):
            halo_copy(side, c).start()
            return 0

        lax.fori_loop(0, chunks, start, 0)

    @pl.when(direct == 0)
    def _():
        start_halo(1 - late)

    start_halo(late)

    own_k.wait()
    zero = jnp.zeros((planes, width), jnp.float32)
    one = jnp.ones((planes, width), jnp.float32)

    def line_row(step, carry):
        v, phi, v_sum, u, psi, u_sum = carry
        for i in range(8):
            j = step * 8 + i
            vs[j] = v
            phi = phi + v
            v_sum = v_sum + v
            v = v + phi * (1.0 / (diffusion_number * ks[pl.ds(j, planes, stride=pitch), :]))
            b = rows - 1 - j
            psi = psi + u
            u = u + psi * (1.0 / (diffusion_number * ks[pl.ds(b, planes, stride=pitch), :]))
            us[b] = u
            u_sum = u_sum + u
        return (v, phi, v_sum, u, psi, u_sum)

    v_end, _, v_sum, u_end, _, u_sum = lax.fori_loop(
        0, rows // 8, line_row, (zero, one, zero, zero, one, zero)
    )
    through = 1.0 / v_end
    norm = 1.0 / u_end
    coef_g[me_w, 0] = through
    coef_g[me_w, 1] = u_sum * norm
    coef_g[me_w, 2] = v_sum * through
    for step in range(1, n_wall):
        wall_copy(coef_g, coef_send, coef_recv, step).start()

    def scale_row(step, _):
        for i in range(8):
            us[step * 8 + i] = us[step * 8 + i] * norm
        return 0

    lax.fori_loop(0, rows // 8, scale_row, 0)
    own_m.wait()

    @pl.when(direct == 1)
    def _():
        start_halo(1 - late)

    def transport(base, first, count):
        at = pl.ds(base, 8)

        def cell(p):
            return [ms[k, first + p + 2, at, :] for k in range(4)]

        below = None
        centre = quadrature(*cell(-2))
        above = quadrature(*cell(-1))
        going = None
        flux_before = None
        for p in range(-1, count + 1):
            below, centre, above = centre, above, quadrature(*cell(p + 1))
            slope = [half_slope(b, c, a) for b, c, a in zip(below, centre, above)]
            if p >= 0:
                coming = directed([c - s for c, s in zip(centre, slope)], False)
                flux = [a + b for a, b in zip(going, coming)]
                if p >= 1:
                    row = pl.ds(pl.multiple_of((first + p - 1) * pitch + base, 8), 8)
                    for k in range(4):
                        ts[k, row, :] = ms[k, first + p + 1, at, :] - courant * (flux[k] - flux_before[k])
                flux_before = flux
            if p < count:
                going = directed([c + s for c, s in zip(centre, slope)], True)

    def add_rows(base, carry, keep):
        sums_v, sums_u = list(carry[:4]), list(carry[4:])
        for i in range(8):
            v = vs[base + i]
            u = us[base + i]
            for k in range(4):
                t = ts[k, pl.ds(base + i, planes, stride=pitch), :]
                sums_v[k] = sums_v[k] + v * t
                sums_u[k] = sums_u[k] + u * t
                if keep:
                    hs[k, base + i] = u * sums_v[k] - v * sums_u[k]
        return tuple(sums_v + sums_u)

    def pass_over(stage):
        first = (1 - late) * 2 if stage == 0 else late * (planes - 2)
        count = planes - 2 if stage == 0 else 2

        def step(c, carry):
            halo_copy(1 - late if stage == 0 else late, c).wait_recv()
            for g in range(chunk // 8):
                base = pl.multiple_of(c * chunk + g * 8, 8)
                transport(base, first, count)
                carry = add_rows(base, carry, stage == 1)
            return carry

        return lax.fori_loop(0, chunks, step, (zero,) * 8)

    def put_sums(sums):
        for k in range(4):
            rhs_g[me_w, pl.ds(k, planes, stride=8), :] = sums[4 + k]
            rhs_g[me_w, pl.ds(4 + k, planes, stride=8), :] = sums[k] * through

    put_sums(pass_over(0))
    for step in range(1, n_wall):
        sums_copy(0, step).start()
    sums = pass_over(1)
    for step in range(1, n_wall):
        sums_copy(0, step).wait()
    put_sums(sums)
    for step in range(1, n_wall):
        sums_copy(1, step).start()
    for step in range(1, n_wall):
        wall_copy(coef_g, coef_send, coef_recv, step).wait()

    links, inverses = [], []
    held = None
    for s in range(n_wall):
        link = coef_g[s, 0]
        ground = coef_g[s, 1]
        if s > 0:
            ground = ground + coef_g[s - 1, 2] + links[-1] * held * inverses[-1]
        held = ground
        links.append(link)
        inverses.append(1.0 / (held + link))

    for step in range(1, n_wall):
        sums_copy(1, step).wait()
    for k in range(4):
        sources = []
        for s in range(n_wall):
            source = rhs_g[s, pl.ds(k, planes, stride=8), :]
            if s > 0:
                source = (
                    source
                    + rhs_g[s - 1, pl.ds(4 + k, planes, stride=8), :]
                    + links[s - 1] * inverses[s - 1] * sources[-1]
                )
            sources.append(source)
        value = zero
        starts[n_wall, k] = zero
        for s in reversed(range(n_wall)):
            value = (sources[s] + links[s] * value) * inverses[s]
            starts[s, k] = value
    for k in range(4):
        ends[k] = starts[me_w, k]
        ends[4 + k] = sums[4 + k] + through * starts[me_w + 1, k]

    def end_halo(c, _):
        halo_copy(0, c).wait_send()
        halo_copy(1, c).wait_send()
        return 0

    lax.fori_loop(0, chunks, end_halo, 0)


def output_kernel(parts, ts, hs, us, vs, ends, t_hbm, x_hbm, xs, t_sem, x_sem):
    planes, rows, width = t_hbm.shape[1], t_hbm.shape[2], t_hbm.shape[3]
    pitch = ts.shape[1] // planes
    size = rows // parts
    moved = pltpu.make_async_copy(
        ts.reshape(4, planes, pitch, width).at[:, :, pl.ds(0, rows), :], t_hbm, t_sem.at[0]
    )
    moved.start()
    copies = []
    for part in range(parts):

        def row_block(step, _):
            for i in range(8):
                j = part * size + step * 8 + i
                v = vs[j]
                u = us[j]
                for k in range(4):
                    xs[k, pl.ds(j, planes, stride=pitch), :] = hs[k, j] + (u * ends[k] + v * ends[4 + k])
            return 0

        lax.fori_loop(0, size // 8, row_block, 0)
        at = pl.ds(part * size, size)
        copy = pltpu.make_async_copy(
            xs.reshape(4, planes, pitch, width).at[:, :, at, :], x_hbm.at[:, :, at, :], x_sem.at[part]
        )
        copy.start()
        copies.append(copy)
    moved.wait()
    for copy in copies:
        copy.wait()


def body(n_span, n_wall, moments, diffusivity):
    _, planes, rows, width = moments.shape
    pitch = rows + 8
    chunk = 16 if rows % 16 == 0 else 8
    f32 = jnp.float32
    dma = pltpu.SemaphoreType.DMA
    any_spec = pl.BlockSpec(memory_space=pl.ANY)
    vmem_spec = pl.BlockSpec(memory_space=pltpu.VMEM)
    middle = [
        (4, planes * pitch, width),
        (4, rows, planes, width),
        (rows, planes, width),
        (rows, planes, width),
        (8, planes, width),
    ]
    held = pl.pallas_call(
        functools.partial(transport_kernel, n_span, n_wall, chunk),
        out_shape=[pltpu.VMEM(shape, f32) for shape in middle],
        in_specs=[pl.BlockSpec(memory_space=pltpu.HBM)] * 2,
        out_specs=[vmem_spec] * 5,
        scratch_shapes=[
            pltpu.VMEM((4, planes + 4, rows, width), f32),
            pltpu.VMEM((planes * pitch, width), f32),
            pltpu.VMEM((n_wall, 3, planes, width), f32),
            pltpu.VMEM((n_wall, planes * 8, width), f32),
            pltpu.VMEM((n_wall + 1, 4, planes, width), f32),
            dma((2,)),
            dma((2, rows // chunk)),
            dma((2, rows // chunk)),
            dma((n_wall - 1,)),
            dma((n_wall - 1,)),
            dma((2, n_wall - 1)),
            dma((2, n_wall - 1)),
        ],
        compiler_params=pltpu.CompilerParams(collective_id=0, has_side_effects=True, vmem_limit_bytes=24 << 20),
        name="transport",
    )(
        pltpu.with_memory_space_constraint(moments, pltpu.HBM),
        pltpu.with_memory_space_constraint(diffusivity, pltpu.HBM),
    )
    parts = 4
    out = jax.ShapeDtypeStruct(moments.shape, f32)
    return pl.pallas_call(
        functools.partial(output_kernel, parts),
        out_shape=[out, out],
        in_specs=[vmem_spec] * 5,
        out_specs=[any_spec, any_spec],
        scratch_shapes=[pltpu.VMEM((4, planes * pitch, width), f32), dma((1,)), dma((parts,))],
        compiler_params=pltpu.CompilerParams(vmem_limit_bytes=24 << 20),
        name="outputs",
    )(*held)


def solution(mesh):
    in_specs = (P(None, "span", "wall", None), P("span", "wall", None))
    out_specs = (P(None, "span", "wall", None), P(None, "span", "wall", None))
    run = functools.partial(body, mesh.shape["span"], mesh.shape["wall"])
    return jax.shard_map(run, mesh=mesh, in_specs=in_specs, out_specs=out_specs, check_vma=False)
```

```python
import functools

import jax
import jax.numpy as jnp
from jax import lax
from jax.experimental import pallas as pl
from jax.experimental.pallas import tpu as pltpu
from jax.sharding import PartitionSpec as P

courant = 0.2
diffusion_number = 20000.0
VMEM_LIMIT = 60 * 1024 * 1024


def quadrature(m0, m1, m2, m3):
    inverse = 1.0 / m0
    mean = m1 * inverse
    ratio_two = m2 * inverse
    central_two = ratio_two - mean * mean
    central_three = m3 * inverse - 3.0 * mean * ratio_two + 2.0 * mean * mean * mean
    half_skew = 0.5 * (central_three / central_two)
    square = half_skew * half_skew + central_two
    inverse_root = lax.rsqrt(square)
    root = square * inverse_root
    scale = m0 * (0.5 * inverse_root)
    low = half_skew - root
    high = half_skew + root
    return (scale * high, -scale * low, mean + low, mean + high)


def half_slope(below, centre, above):
    first = above - centre
    second = centre - below
    return 0.5 * (
        jnp.maximum(jnp.minimum(first, second), 0.0) + jnp.minimum(jnp.maximum(first, second), 0.0)
    )


def directed(state, outgoing):
    total = None
    for node in range(2):
        speed = state[node + 2]
        carried = jnp.maximum(speed, 0.0) if outgoing else jnp.minimum(speed, 0.0)
        term = state[node] * carried
        terms = [term]
        for _ in range(3):
            term = term * speed
            terms.append(term)
        total = terms if total is None else [a + b for a, b in zip(total, terms)]
    return total


def transport_kernel(
    n_span, n_wall, chunk,
    m_hbm, k_hbm,
    ts, xs, un, vn, ends,
    ms, ks, hs, us, vs, coef_g, rhs_g, last_g, starts,
    own_sem, halo_send, halo_recv, coef_send, coef_recv, rhs_send, rhs_recv,
):
    planes, rows, width = m_hbm.shape[1], m_hbm.shape[2], m_hbm.shape[3]
    pitch = ts.shape[1] // planes
    chunks = rows // chunk
    me_s = lax.axis_index("span")
    me_w = lax.axis_index("wall")
    right = lax.rem(me_s + 1, n_span)
    left = lax.rem(me_s + n_span - 1, n_span)
    late = lax.rem(me_s, 2)

    own_k = pltpu.make_async_copy(k_hbm, ks.reshape(planes, pitch, width).at[:, pl.ds(0, rows), :], own_sem.at[0])
    own_k.start()
    own_m = pltpu.make_async_copy(m_hbm, ms.at[:, pl.ds(2, planes)], own_sem.at[1])
    own_m.start()

    barrier = pltpu.get_barrier_semaphore()
    for other in (left, right):
        pl.semaphore_signal(barrier, inc=1, device_id={"span": other}, device_id_type=pl.DeviceIdType.MESH)
    for step in range(1, n_wall):
        pl.semaphore_signal(
            barrier, inc=1, device_id={"wall": lax.rem(me_w + step, n_wall)}, device_id_type=pl.DeviceIdType.MESH
        )
    pl.semaphore_wait(barrier, n_wall + 1)

    def halo_copy(side, c):
        at = pl.ds(pl.multiple_of(c * chunk, 8), chunk)
        return pltpu.make_async_remote_copy(
            src_ref=m_hbm.at[:, pl.ds((1 - side) * (planes - 2), 2), at, :],
            dst_ref=ms.at[:, pl.ds(side * (planes + 2), 2), at, :],
            send_sem=halo_send.at[side, c],
            recv_sem=halo_recv.at[side, c],
            device_id={"span": lax.rem(me_s + 1 + side * (n_span - 2), n_span)},
            device_id_type=pl.DeviceIdType.MESH,
        )

    def wall_copy(buffer, send, recv, step, *at):
        part = buffer.at[(me_w, *at)]
        return pltpu.make_async_remote_copy(
            src_ref=part,
            dst_ref=part,
            send_sem=send.at[step - 1],
            recv_sem=recv.at[step - 1],
            device_id={"wall": lax.rem(me_w + step, n_wall)},
            device_id_type=pl.DeviceIdType.MESH,
        )

    def sums_copy(stage, step):
        return wall_copy(rhs_g if stage == 0 else last_g, rhs_send.at[stage], rhs_recv.at[stage], step)

    direct = lax.rem(lax.div(me_s, 2) + me_s, 2)

    def start_halo(side):
        def start(c, _):
            halo_copy(side, c).start()
            return 0

        lax.fori_loop(0, chunks, start, 0)

    @pl.when(direct == 0)
    def _():
        start_halo(1 - late)

    start_halo(late)

    own_k.wait()
    zero = jnp.zeros((planes, width), jnp.float32)
    one = jnp.ones((planes, width), jnp.float32)

    def line_row(step, carry):
        v, phi, v_sum, u, psi, u_sum = carry
        for i in range(8):
            j = step * 8 + i
            vs[j] = v
            phi = phi + v
            v_sum = v_sum + v
            v = v + phi * (1.0 / (diffusion_number * ks[pl.ds(j, planes, stride=pitch), :]))
            b = rows - 1 - j
            psi = psi + u
            u = u + psi * (1.0 / (diffusion_number * ks[pl.ds(b, planes, stride=pitch), :]))
            us[b] = u
            u_sum = u_sum + u
        return (v, phi, v_sum, u, psi, u_sum)

    v_end, _, v_sum, u_end, _, u_sum = lax.fori_loop(
        0, rows // 8, line_row, (zero, one, zero, zero, one, zero)
    )
    through = 1.0 / v_end
    norm = 1.0 / u_end
    coef_g[me_w, 0] = through
    coef_g[me_w, 1] = u_sum * norm
    coef_g[me_w, 2] = v_sum * through
    for step in range(1, n_wall):
        wall_copy(coef_g, coef_send, coef_recv, step).start()

    def scale_row(step, _):
        for i in range(8):
            us[step * 8 + i] = us[step * 8 + i] * norm
        return 0

    lax.fori_loop(0, rows // 8, scale_row, 0)
    own_m.wait()

    @pl.when(direct == 1)
    def _():
        start_halo(1 - late)

    def transport(base, first, count):
        at = pl.ds(base, 8)

        def cell(p):
            return [ms[k, first + p + 2, at, :] for k in range(4)]

        below = None
        centre = quadrature(*cell(-2))
        above = quadrature(*cell(-1))
        going = None
        flux_before = None
        for p in range(-1, count + 1):
            below, centre, above = centre, above, quadrature(*cell(p + 1))
            slope = [half_slope(b, c, a) for b, c, a in zip(below, centre, above)]
            if p >= 0:
                coming = directed([c - s for c, s in zip(centre, slope)], False)
                flux = [a + b for a, b in zip(going, coming)]
                if p >= 1:
                    row = pl.ds(pl.multiple_of((first + p - 1) * pitch + base, 8), 8)
                    for k in range(4):
                        ts[k, row, :] = ms[k, first + p + 1, at, :] - courant * (flux[k] - flux_before[k])
                flux_before = flux
            if p < count:
                going = directed([c + s for c, s in zip(centre, slope)], True)

    def add_rows(base, carry, keep):
        sums_v, sums_u = list(carry[:4]), list(carry[4:])
        for i in range(8):
            v = vs[base + i]
            u = us[base + i]
            for k in range(4):
                t = ts[k, pl.ds(base + i, planes, stride=pitch), :]
                sums_v[k] = sums_v[k] + v * t
                sums_u[k] = sums_u[k] + u * t
                if keep:
                    hs[k, base + i] = u * sums_v[k] - v * sums_u[k]
        return tuple(sums_v + sums_u)

    def pass_over(stage):
        first = (1 - late) * 2 if stage == 0 else late * (planes - 2)
        count = planes - 2 if stage == 0 else 2

        def step(c, carry):
            halo_copy(1 - late if stage == 0 else late, c).wait_recv()
            for g in range(chunk // 8):
                base = pl.multiple_of(c * chunk + g * 8, 8)
                transport(base, first, count)
                carry = add_rows(base, carry, stage == 1)
            return carry

        return lax.fori_loop(0, chunks, step, (zero,) * 8)

    def put_sums(sums):
        for k in range(4):
            rhs_g[me_w, pl.ds(k, planes, stride=8), :] = sums[4 + k]
            rhs_g[me_w, pl.ds(4 + k, planes, stride=8), :] = sums[k] * through

    put_sums(pass_over(0))
    for step in range(1, n_wall):
        sums_copy(0, step).start()
    sums = pass_over(1)
    for step in range(1, n_wall):
        sums_copy(0, step).wait()
    put_sums(sums)
    late_rows = pl.ds(pl.multiple_of(late * 8 * (planes - 2), 8), 16)
    last_g[me_w] = rhs_g[me_w, late_rows, :]
    for step in range(1, n_wall):
        sums_copy(1, step).start()
    for step in range(1, n_wall):
        wall_copy(coef_g, coef_send, coef_recv, step).wait()

    links, inverses = [], []
    held = None
    for s in range(n_wall):
        link = coef_g[s, 0]
        ground = coef_g[s, 1]
        if s > 0:
            ground = ground + coef_g[s - 1, 2] + links[-1] * held * inverses[-1]
        held = ground
        links.append(link)
        inverses.append(1.0 / (held + link))

    def solve_ends():
        for k in range(4):
            sources = []
            for s in range(n_wall):
                source = rhs_g[s, pl.ds(k, planes, stride=8), :]
                if s > 0:
                    source = (
                        source
                        + rhs_g[s - 1, pl.ds(4 + k, planes, stride=8), :]
                        + links[s - 1] * inverses[s - 1] * sources[-1]
                    )
                sources.append(source)
            value = zero
            starts[n_wall, k] = zero
            for s in reversed(range(n_wall)):
                value = (sources[s] + links[s] * value) * inverses[s]
                starts[s, k] = value
        for k in range(4):
            ends[k] = starts[me_w, k]
            ends[4 + k] = sums[4 + k] + through * starts[me_w + 1, k]

    solve_ends()
    plane = lax.broadcasted_iota(jnp.int32, (planes, width), 0)
    first_late = late * (planes - 2)
    early = jnp.logical_or(plane < first_late, plane >= first_late + 2)
    known = [jnp.where(early, ends[k], 0.0) for k in range(8)]

    def early_rows(step, _):
        for i in range(8):
            j = step * 8 + i
            at = pl.ds(j, planes, stride=pitch)
            v = vs[j]
            u = us[j]
            un[at, :] = u
            vn[at, :] = v
            for k in range(4):
                xs[k, at, :] = hs[k, j] + (u * known[k] + v * known[4 + k])
        return 0

    lax.fori_loop(0, rows // 8, early_rows, 0)
    for step in range(1, n_wall):
        sums_copy(1, step).wait()
    for s in range(n_wall):
        rhs_g[s, late_rows, :] = last_g[s]
    solve_ends()

    def end_halo(c, _):
        halo_copy(0, c).wait_send()
        halo_copy(1, c).wait_send()
        return 0

    lax.fori_loop(0, chunks, end_halo, 0)


def output_kernel(ts, xs, un, vn, ends, t_hbm, x_hbm, last, t_sem, x_sem):
    planes, rows, width = t_hbm.shape[1], t_hbm.shape[2], t_hbm.shape[3]
    pitch = ts.shape[1] // planes
    late = lax.rem(lax.axis_index("span"), 2)
    early = pl.ds((1 - late) * 2, planes - 2)
    first = late * (planes - 2)
    whole = (4, planes, pitch, width)
    copies = [
        pltpu.make_async_copy(xs.reshape(whole).at[:, early, pl.ds(0, rows), :], x_hbm.at[:, early], x_sem.at[0]),
        pltpu.make_async_copy(ts.reshape(whole).at[:, :, pl.ds(0, rows), :], t_hbm, t_sem.at[0]),
    ]
    for copy in copies:
        copy.start()
    for p in range(2):
        lows = [jnp.broadcast_to(ends[k, pl.ds(first + p, 1), :], (8, width)) for k in range(8)]
        for block in range(rows // 8):
            at = pl.ds(pl.multiple_of((first + p) * pitch + block * 8, 8), 8)
            u = un[at, :]
            v = vn[at, :]
            for k in range(4):
                last[k, p, pl.ds(block * 8, 8), :] = xs[k, at, :] + (u * lows[k] + v * lows[4 + k])
    copy = pltpu.make_async_copy(last, x_hbm.at[:, pl.ds(first, 2)], x_sem.at[1])
    copy.start()
    for other in copies + [copy]:
        other.wait()


def body(n_span, n_wall, moments, diffusivity):
    _, planes, rows, width = moments.shape
    pitch = rows + 8
    chunk = 16 if rows % 16 == 0 else 8
    f32 = jnp.float32
    dma = pltpu.SemaphoreType.DMA
    any_spec = pl.BlockSpec(memory_space=pl.ANY)
    vmem_spec = pl.BlockSpec(memory_space=pltpu.VMEM)
    middle = [
        (4, planes * pitch, width),
        (4, planes * pitch, width),
        (planes * pitch, width),
        (planes * pitch, width),
        (8, planes, width),
    ]
    held = pl.pallas_call(
        functools.partial(transport_kernel, n_span, n_wall, chunk),
        out_shape=[pltpu.VMEM(shape, f32) for shape in middle],
        in_specs=[pl.BlockSpec(memory_space=pltpu.HBM)] * 2,
        out_specs=[vmem_spec] * 5,
        scratch_shapes=[
            pltpu.VMEM((4, planes + 4, rows, width), f32),
            pltpu.VMEM((planes * pitch, width), f32),
            pltpu.VMEM((4, rows, planes, width), f32),
            pltpu.VMEM((rows, planes, width), f32),
            pltpu.VMEM((rows, planes, width), f32),
            pltpu.VMEM((n_wall, 3, planes, width), f32),
            pltpu.VMEM((n_wall, planes * 8, width), f32),
            pltpu.VMEM((n_wall, 16, width), f32),
            pltpu.VMEM((n_wall + 1, 4, planes, width), f32),
            dma((2,)),
            dma((2, rows // chunk)),
            dma((2, rows // chunk)),
            dma((n_wall - 1,)),
            dma((n_wall - 1,)),
            dma((2, n_wall - 1)),
            dma((2, n_wall - 1)),
        ],
        compiler_params=pltpu.CompilerParams(collective_id=0, has_side_effects=True, vmem_limit_bytes=24 << 20),
        name="transport",
    )(
        pltpu.with_memory_space_constraint(moments, pltpu.HBM),
        pltpu.with_memory_space_constraint(diffusivity, pltpu.HBM),
    )
    out = jax.ShapeDtypeStruct(moments.shape, f32)
    return pl.pallas_call(
        output_kernel,
        out_shape=[out, out],
        in_specs=[vmem_spec] * 5,
        out_specs=[any_spec, any_spec],
        scratch_shapes=[pltpu.VMEM((4, 2, rows, width), f32), dma((1,)), dma((2,))],
        compiler_params=pltpu.CompilerParams(vmem_limit_bytes=24 << 20),
        name="outputs",
    )(*held)


def solution(mesh):
    in_specs = (P(None, "span", "wall", None), P("span", "wall", None))
    out_specs = (P(None, "span", "wall", None), P(None, "span", "wall", None))
    run = functools.partial(body, mesh.shape["span"], mesh.shape["wall"])
    return jax.shard_map(run, mesh=mesh, in_specs=in_specs, out_specs=out_specs, check_vma=False)
```
